32 devices in a mesh: prow: 2 (over y), pcol: 16 (over z, x, core).
Axes of the slice: x: 2, y: 2, z: 4, core: 2. Of those that a mesh axis runs over, the one named last changes fastest.
Arguments:
- matrix: float32 [32, 2, 256, 4, 16, 256], P(None, 'prow', None, None, 'pcol'), may hold values from -6 to 6
- inverses: float32 [3, 256, 256], replicated, as said below
Outputs:
- factored: float32 [32, 2, 256, 4, 16, 256], P(None, 'prow', None, None, 'pcol')
The draws below stay inside these ranges and needn't reach their ends.
Inputs may be any that keep to these rules, and one draw needn't show every extreme that they name: Each of the 3 matrices of inverses is lower triangular with a positive diagonal.
All inputs are finite; a program needn't handle non-finite values.
Results may differ from the reference program's by a relative error of at most 0.0003.
Values sent between devices are 32-bit elements; how exact they have to be, the bound alone decides.
A program may use at most 256 MiB of HBM per device.

```python
import math
import jax
import jax.numpy as jnp
from jax import lax

N = 16384
NB = 256
STEPS = 3
RB = 32
CB = 4
N_PROW = 2
N_PCOL = 16


def draw_inverses(key, part):
    key_diag = jax.random.fold_in(key, 11)
    key_lower = jax.random.fold_in(key, 23)
    spread = 0.1 / math.sqrt(NB)
    diagonal = jax.random.uniform(key_diag, (STEPS, NB), jnp.float32, 0.13, 0.19)
    lower_part = jax.random.normal(key_lower, (STEPS, NB, NB), jnp.float32) * spread
    row_ids = jnp.arange(NB)[:, None]
    col_ids = jnp.arange(NB)[None, :]
    strict = jnp.where((row_ids > col_ids)[None], lower_part, 0.0)
    return strict + jnp.eye(NB, dtype=jnp.float32)[None] * diagonal[:, :, None]


def shard_levels(key, extent, pieces, least, top_value):
    def one(axis_at, parts):
        heights = jax.random.uniform(jax.random.fold_in(jax.random.fold_in(key, 6), axis_at), (parts,), jnp.float32, least / len(pieces), top_value / len(pieces))
        return jnp.repeat(jnp.exp(heights), extent[axis_at] // parts).reshape((-1,) + (1,) * (len(extent) - axis_at - 1))

    loudness = one(*pieces[0])
    for cut in pieces[1:]:
        loudness = loudness * one(*cut)
    return loudness


def bell_draw(key, dims, scale, most, split=(), held_as=jnp.bfloat16):
    drawn = jax.random.normal(key, dims, jnp.float32) * scale
    if len(split) > 0:
        drawn = shard_levels(key, dims, split, -0.22, 0.18) * drawn
    return jnp.clip(drawn, min=-most, max=most).astype(held_as)


def setup_inputs(seed: int = 0) -> dict:
    arg_keys = jax.random.split(jax.random.key(seed), 3)
    return {
        "matrix": bell_draw(arg_keys[0], (RB, N_PROW, NB, CB, N_PCOL, NB), 1.0, 6.0, ((1, 2), (4, 16)), jnp.float32),
        "inverses": draw_inverses(jax.random.fold_in(arg_keys[2], 71), 0),
    }


exact_precision = lax.Precision.HIGHEST


def reference(matrix, inverses):
    blocks_total = N // NB
    by_columns = matrix.transpose(3, 4, 0, 1, 2, 5).reshape(blocks_total, N, NB)
    row_index = jnp.arange(N, dtype=jnp.int32)
    for factor_step in range(STEPS):
        lower_edge = factor_step * NB
        upper_edge = lower_edge + NB
        column = by_columns[factor_step]
        panel = jnp.dot(column, inverses[factor_step].T, precision=exact_precision, preferred_element_type=jnp.float32)
        panel = jnp.where((row_index >= lower_edge)[:, None], panel, jnp.float32(0.0))

        def update_block(pair):
            block_values, block_index = pair
            partner = lax.dynamic_slice_in_dim(panel, (block_index * NB).astype(jnp.int32), NB, 0)
            product = jnp.dot(panel, partner.T, precision=exact_precision, preferred_element_type=jnp.float32)
            live_mask = (row_index >= upper_edge)[:, None] & (block_index > factor_step)
            return jnp.where(live_mask, block_values - product, block_values)

        by_columns = lax.map(update_block, (by_columns, jnp.arange(blocks_total, dtype=jnp.int32)))
        by_columns = by_columns.at[factor_step].set(panel)
    block_ids = jnp.arange(blocks_total, dtype=jnp.int32)
    col_index = block_ids[:, None] * NB + jnp.arange(NB, dtype=jnp.int32)[None, :]
    kept_mask = (row_index[None, :, None] >= col_index[:, None, :]) | (block_ids < STEPS)[:, None, None]
    by_columns = jnp.where(kept_mask, by_columns, jnp.float32(0.0))
    return by_columns.reshape(CB, N_PCOL, RB, N_PROW, NB, NB).transpose(2, 3, 4, 0, 1, 5)
```

```python
import functools

import jax
import jax.numpy as jnp
from jax import lax
from jax.experimental import pallas as pl
from jax.experimental.pallas import tpu as pltpu
from jax.sharding import PartitionSpec as P

STEPS = 3
WINDOW = 4
LAG = 2
MESH = pl.DeviceIdType.MESH
BF = jnp.bfloat16
F32 = jnp.float32


def split(value):
    high = value.astype(BF)
    return high, (value - high.astype(F32)).astype(BF)


def dot_nt(a, b):
    return lax.dot_general(a, b, (((1,), (1,)), ((), ())), preferred_element_type=F32)


def dot3(a, b):
    return dot_nt(a[0], b[0]) + (dot_nt(a[0], b[1]) + dot_nt(a[1], b[0]))


def kernel(
    n_prow, n_pcol, rb, cb, nb,
    a_hbm, src_hbm, inv_ref, out_hbm,
    panels, xch, abuf, obuf, cst, chi, clo, prow_f, prow_h,
    rsem, ssem, xrsem, xssem, asem, osem, lsem,
):
    p = lax.axis_index("prow")
    q = lax.axis_index("pcol")
    depth = n_pcol // 4
    z, x, c = q // 4, (q // 2) % 2, q % 2
    sib = q + 1 - 2 * c
    xn = q + 2 - 4 * x
    quarter = nb // 4
    lines = nb * cb * 2
    stride = cb * 2
    slots = 2 + cb

    barrier = pltpu.get_barrier_semaphore()

    def greet(pp, qq):
        pl.semaphore_signal(barrier, inc=1, device_id=(pp, qq), device_id_type=MESH)

    greet(p, sib)
    greet(p, xn)
    pl.when(z > 0)(lambda: greet(p, q - 4))
    pl.when(z < depth - 1)(lambda: greet(p, q + 4))
    for d in range(1, n_prow):
        greet((p + d) % n_prow, q)
    peers = 1 + n_prow + (z > 0).astype(jnp.int32) + (z < depth - 1).astype(jnp.int32)
    pl.semaphore_wait(barrier, peers)

    def cp_q(a, j, dev, si, ri):
        ref = panels.at[a, :, pl.ds(pl.multiple_of(j * quarter, quarter), quarter), :]
        return pltpu.make_async_remote_copy(
            src_ref=ref, dst_ref=ref, send_sem=ssem.at[a % WINDOW, si], recv_sem=rsem.at[a, ri],
            device_id=(p, dev), device_id_type=MESH,
        )

    def cp_k(a, k, dev, si):
        ref = panels.at[a, k]
        return pltpu.make_async_remote_copy(
            src_ref=ref, dst_ref=ref, send_sem=ssem.at[a % WINDOW, si], recv_sem=rsem.at[a, k],
            device_id=(p, dev), device_id_type=MESH,
        )

    mine = 2 * x + c
    other = 2 * (1 - x) + c
    send_z = lambda a: cp_q(a, mine, jnp.minimum(q + 4, n_pcol - 1), 0, 0)
    send_x = lambda a: cp_q(a, mine, xn, 1, 1)
    send_c1 = lambda a: cp_q(a, mine, sib, 2, 2)
    send_c2 = lambda a: cp_q(a, other, sib, 3, 3)
    recv_z = lambda a: cp_q(a, mine, sib, 0, 0)
    recv_x = lambda a: cp_q(a, other, sib, 1, 1)
    recv_c1 = lambda a: cp_q(a, 2 * x + 1 - c, sib, 2, 2)
    recv_c2 = lambda a: cp_q(a, 2 * (1 - x) + 1 - c, sib, 3, 3)

    def start(fn, a):
        @pl.when(a >= WINDOW)
        def _():
            fn(a - WINDOW).wait_send()
        fn(a).start()

    def drain(fn):
        for a in range(max(rb - WINDOW, 0), rb):
            fn(a).wait_send()

    def fwd_of(k):
        return k + 2 - 4 * ((k // 2) % 2)

    def block_of(s):
        return s + 1 if s < 2 else (s - 2) * n_pcol + q

    def cp_x(s, a, d):
        return pltpu.make_async_remote_copy(
            src_ref=panels.at[a], dst_ref=xch.at[s], send_sem=xssem.at[s, d], recv_sem=xrsem.at[s],
            device_id=((p + d) % n_prow, q), device_id_type=MESH,
        )

    def cp_l(s, a):
        return pltpu.make_async_copy(panels.at[a], xch.at[s], xrsem.at[s])

    def publish(a):
        for s in range(slots):
            g = block_of(s)

            @pl.when((g % n_prow == p) & (g // n_prow == a))
            def _():
                for d in range(1, n_prow):
                    cp_x(s, a, d).start()
                cp_l(s, a).start()

    def wait_slot(s):
        g = block_of(s)

        @pl.when(g % n_prow == p)
        def _():
            cp_l(s, 0).wait()

        @pl.when(g % n_prow != p)
        def _():
            cp_x(s, 0, 1).wait_recv()

    for k in range(STEPS):
        @pl.when(q == k)
        def _():
            copy = pltpu.make_async_copy(src_hbm, panels.at[:, k], lsem)
            copy.start()
            copy.wait()

    def a_in(a):
        return pltpu.make_async_copy(
            a_hbm.at[pl.ds(pl.multiple_of(a * lines, lines), lines), :], abuf.at[a % 2], asem.at[a % 2])

    def o_out(a):
        return pltpu.make_async_copy(
            obuf.at[a % 2], out_hbm.at[pl.ds(pl.multiple_of(a * lines, lines), lines), :], osem.at[a % 2])

    a_in(0).start()

    def const(i):
        return cst[0, i], cst[1, i]

    def solve(ref):
        p0 = dot3(split(ref[0]), const(0))
        s0 = split(p0)
        p1 = dot3(split(ref[1] - dot3(s0, const(3))), const(1))
        s1 = split(p1)
        p2 = dot3(split(ref[2] - dot3(s0, const(4)) - dot3(s1, const(5))), const(2))
        return p0, p1, p2

    def set_const(i, value):
        h, l = split(value)
        cst[0, i] = h
        cst[1, i] = l

    def compute(a):
        g = a * n_prow + p

        @pl.when(a + 1 < rb)
        def _():
            a_in(a + 1).start()

        @pl.when(a == 0)
        def _():
            wait_slot(0)
            wait_slot(1)
            for k in range(STEPS):
                set_const(k, inv_ref[k])
            set_const(3, dot3(split(xch[0, 0]), const(0)))
            set_const(4, dot3(split(xch[1, 0]), const(0)))
            set_const(5, dot3(split(xch[1, 1] - dot3(const(4), const(3))), const(1)))

        parts = solve(panels.at[a])
        for k in range(STEPS):
            v = jnp.where(g >= k, parts[k], 0.0)
            prow_f[k] = v
            h, l = split(v)
            prow_h[0, :, k * nb:(k + 1) * nb] = h
            prow_h[1, :, k * nb:(k + 1) * nb] = l

        for b in range(cb):
            gb = block_of(2 + b)
            first = jnp.minimum((gb - p + n_prow - 1) // n_prow, rb - 1)

            @pl.when(a == first)
            def _():
                wait_slot(2 + b)
                cols = solve(xch.at[2 + b])
                for k in range(STEPS):
                    h, l = split(cols[k])
                    chi[b, :, k * nb:(k + 1) * nb] = h
                    clo[b, :, k * nb:(k + 1) * nb] = l

        @pl.when(a >= 2)
        def _():
            o_out(a - 2).wait()
        a_in(a).wait()
        par = a % 2
        for b in range(cb):
            gb = block_of(2 + b)

            def put(value):
                for h in range(2):
                    obuf[par, pl.ds(b * 2 + h, nb, stride=stride), :] = value[:, h * 128:(h + 1) * 128]

            def updated():
                old = jnp.concatenate(
                    [abuf[par, pl.ds(b * 2 + h, nb, stride=stride), :] for h in range(2)], axis=1)
                return old - dot3((prow_h[0], prow_h[1]), (chi[b], clo[b]))

            @pl.when((gb >= STEPS) & (g > gb))
            def _():
                put(updated())

            @pl.when((gb >= STEPS) & (g == gb))
            def _():
                rows = lax.broadcasted_iota(jnp.int32, (nb, nb), 0)
                cols = lax.broadcasted_iota(jnp.int32, (nb, nb), 1)
                put(jnp.where(rows >= cols, updated(), 0.0))

            @pl.when((gb >= STEPS) & (g < gb))
            def _():
                put(jnp.zeros((nb, nb), F32))

            if b == 0:
                for k in range(STEPS):
                    @pl.when(gb == k)
                    def _():
                        put(prow_f[k])
        o_out(a).start()

    def step(t, carry):
        @pl.when(t < rb)
        def _():
            a = t

            @pl.when(z > 0)
            def _():
                recv_z(a).wait_recv()
                pl.when(z < depth - 1)(lambda: start(send_z, a))
                start(send_x, a)
                start(send_c1, a)

            for k in range(STEPS):
                @pl.when(q == k)
                def _():
                    start(lambda i: cp_k(i, k, xn, 1 + 2 * k), a)
                    start(lambda i: cp_k(i, k, sib, 2 + 2 * k), a)

        @pl.when((t >= 1) & (t < rb + 1))
        def _():
            a = t - 1

            @pl.when(z > 0)
            def _():
                recv_x(a).wait_recv()
                start(send_c2, a)

            for k in range(STEPS):
                @pl.when(q == fwd_of(k))
                def _():
                    cp_k(a, k, sib, 1 + 2 * k).wait_recv()
                    start(lambda i: cp_k(i, k, sib, 1 + 2 * k), a)

        @pl.when((t >= 2) & (t < rb + 2))
        def _():
            a = t - 2

            @pl.when(z > 0)
            def _():
                recv_c1(a).wait_recv()
                recv_c2(a).wait_recv()

            @pl.when(z == 0)
            def _():
                for k in range(STEPS):
                    @pl.when((q != k) & (q != fwd_of(k)))
                    def _():
                        cp_k(a, k, sib, 1 + 2 * k).wait_recv()
                if depth > 1:
                    start(send_z, a)

            publish(a)

        @pl.when(t >= 2 + LAG)
        def _():
            compute(t - 2 - LAG)

        return carry

    lax.fori_loop(0, rb + 2 + LAG, step, 0)

    pl.when(z < depth - 1)(lambda: drain(send_z))

    @pl.when(z > 0)
    def _():
        drain(send_x)
        drain(send_c1)
        drain(send_c2)

    for k in range(STEPS):
        @pl.when(q == k)
        def _():
            drain(lambda i: cp_k(i, k, xn, 1 + 2 * k))
            drain(lambda i: cp_k(i, k, sib, 2 + 2 * k))

        @pl.when(q == fwd_of(k))
        def _():
            drain(lambda i: cp_k(i, k, sib, 1 + 2 * k))
    for s in range(slots):
        @pl.when(block_of(s) % n_prow == p)
        def _():
            for d in range(1, n_prow):
                cp_x(s, 0, d).wait_send()
    for a in range(max(rb - 2, 0), rb):
        o_out(a).wait()


def per_device(n_prow, n_pcol, matrix, inverses):
    rb, _, nb, cb, _, _ = matrix.shape
    lines = matrix.reshape(rb * nb * cb * 2, nb // 2)
    source = matrix[:, 0, :, 0, 0, :]
    vmem = pltpu.VMEM
    dma = pltpu.SemaphoreType.DMA
    out = pl.pallas_call(
        functools.partial(kernel, n_prow, n_pcol, rb, cb, nb),
        out_shape=jax.ShapeDtypeStruct(lines.shape, F32),
        in_specs=[
            pl.BlockSpec(memory_space=pl.ANY),
            pl.BlockSpec(memory_space=pl.ANY),
            pl.BlockSpec(memory_space=pltpu.VMEM),
        ],
        out_specs=pl.BlockSpec(memory_space=pl.ANY),
        scratch_shapes=[
            vmem((rb, STEPS, nb, nb), F32),
            vmem((2 + cb, STEPS, nb, nb), F32),
            vmem((2, nb * cb * 2, 128), F32),
            vmem((2, nb * cb * 2, 128), F32),
            vmem((2, 6, nb, nb), BF),
            vmem((cb, nb, STEPS * nb), BF),
            vmem((cb, nb, STEPS * nb), BF),
            vmem((STEPS, nb, nb), F32),
            vmem((2, nb, STEPS * nb), BF),
            dma((rb, 4)),
            dma((WINDOW, 8)),
            dma((2 + cb,)),
            dma((2 + cb, n_prow)),
            dma((2,)),
            dma((2,)),
            dma,
        ],
        compiler_params=pltpu.CompilerParams(
            collective_id=0, has_side_effects=True, vmem_limit_bytes=58 * 1024 * 1024
        ),
    )(lines, source, inverses)
    return out.reshape(matrix.shape)


def solution(mesh):
    in_specs = (P(None, "prow", None, None, "pcol", None), P())
    out_specs = P(None, "prow", None, None, "pcol", None)
    return jax.shard_map(
        functools.partial(per_device, mesh.shape["prow"], mesh.shape["pcol"]),
        mesh=mesh, in_specs=in_specs, out_specs=out_specs, check_vma=False,
    )
```

```python
import functools

import jax
import jax.numpy as jnp
from jax import lax
from jax.experimental import pallas as pl
from jax.experimental.pallas import tpu as pltpu
from jax.sharding import PartitionSpec as P

STEPS = 3
WINDOW = 4
LAG = 2
BACK = 3
MESH = pl.DeviceIdType.MESH
BF = jnp.bfloat16
F32 = jnp.float32


def split(value):
    high = value.astype(BF)
    return high, (value - high.astype(F32)).astype(BF)


def dot_nt(a, b):
    return lax.dot_general(a, b, (((1,), (1,)), ((), ())), preferred_element_type=F32)


def dot3(a, b):
    return dot_nt(a[0], b[0]) + (dot_nt(a[0], b[1]) + dot_nt(a[1], b[0]))


def kernel(
    n_prow, n_pcol, rb, cb, nb,
    a_hbm, inv_ref, out_hbm,
    panels, xch, sbuf, abuf, obuf, cst, chi, clo, prow_f, prow_h,
    rsem, ssem, xrsem, xssem, asem, osem, srcsem,
):
    p = lax.axis_index("prow")
    q = lax.axis_index("pcol")
    depth = n_pcol // 4
    z, x, c = q // 4, (q // 2) % 2, q % 2
    sib = q + 1 - 2 * c
    xn = q + 2 - 4 * x
    quarter = nb // 4
    lines = nb * cb * 2
    stride = cb * 2
    slots = 2 + cb

    barrier = pltpu.get_barrier_semaphore()

    def greet(pp, qq):
        pl.semaphore_signal(barrier, inc=1, device_id=(pp, qq), device_id_type=MESH)

    greet(p, sib)
    greet(p, xn)
    pl.when(z > 0)(lambda: greet(p, q - 4))
    pl.when(z < depth - 1)(lambda: greet(p, q + 4))
    for d in range(1, n_prow):
        greet((p + d) % n_prow, q)
    peers = 1 + n_prow + (z > 0).astype(jnp.int32) + (z < depth - 1).astype(jnp.int32)
    pl.semaphore_wait(barrier, peers)

    def cp_q(a, j, dev, si, ri):
        ref = panels.at[a, :, pl.ds(pl.multiple_of(j * quarter, quarter), quarter), :]
        return pltpu.make_async_remote_copy(
            src_ref=ref, dst_ref=ref, send_sem=ssem.at[a % WINDOW, si], recv_sem=rsem.at[a, ri],
            device_id=(p, dev), device_id_type=MESH,
        )

    def cp_k(a, k, dev, si):
        ref = panels.at[a, k]
        return pltpu.make_async_remote_copy(
            src_ref=ref, dst_ref=ref, send_sem=ssem.at[a % WINDOW, si], recv_sem=rsem.at[a, k],
            device_id=(p, dev), device_id_type=MESH,
        )

    mine = 2 * x + c
    other = 2 * (1 - x) + c
    send_z = lambda a: cp_q(a, mine, jnp.minimum(q + 4, n_pcol - 1), 0, 0)
    send_x = lambda a: cp_q(a, mine, xn, 1, 1)
    send_c1 = lambda a: cp_q(a, mine, sib, 2, 2)
    send_c2 = lambda a: cp_q(a, other, sib, 3, 3)
    recv_z = lambda a: cp_q(a, mine, sib, 0, 0)
    recv_x = lambda a: cp_q(a, other, sib, 1, 1)
    recv_c1 = lambda a: cp_q(a, 2 * x + 1 - c, sib, 2, 2)
    recv_c2 = lambda a: cp_q(a, 2 * (1 - x) + 1 - c, sib, 3, 3)

    def cp_half(a, dev):
        ref = panels.at[a, 0, pl.ds(nb // 2, nb // 2), :]
        return pltpu.make_async_remote_copy(
            src_ref=ref, dst_ref=ref, send_sem=ssem.at[a % WINDOW, 1], recv_sem=rsem.at[a, 0],
            device_id=(p, dev), device_id_type=MESH,
        )

    def cp_dn(a, j, dev, si, ri):
        ref = panels.at[a, 0, pl.ds(pl.multiple_of(j * quarter, quarter), quarter), :]
        return pltpu.make_async_remote_copy(
            src_ref=ref, dst_ref=ref, send_sem=ssem.at[a % WINDOW, si], recv_sem=rsem.at[a, ri],
            device_id=(p, dev), device_id_type=MESH,
        )

    low = (z == 0) & (x == 1)
    above = (z == 1) & (x == 1)
    send_dn = lambda a: cp_dn(a, c, jnp.maximum(q - 4, 0), 4, 3)
    recv_dn = lambda a: cp_dn(a, c, sib, 4, 3)
    send_dc = lambda a: cp_dn(a, c, sib, 7, 4)
    recv_dc = lambda a: cp_dn(a, 1 - c, sib, 7, 4)

    def to_x(k):
        return (lambda i: cp_half(i, xn)) if k == 0 else (lambda i: cp_k(i, k, xn, 1 + 2 * k))

    def to_sib(k):
        return lambda i: cp_k(i, k, sib, 2 + 2 * k)

    def fwd(k):
        return (lambda i: cp_half(i, sib)) if k == 0 else (lambda i: cp_k(i, k, sib, 1 + 2 * k))

    def start(fn, a):
        @pl.when(a >= WINDOW)
        def _():
            fn(a - WINDOW).wait_send()
        fn(a).start()

    def drain(fn):
        for a in range(max(rb - WINDOW, 0), rb):
            fn(a).wait_send()

    def fwd_of(k):
        return k + 2 - 4 * ((k // 2) % 2)

    def block_of(s):
        return s + 1 if s < 2 else (s - 2) * n_pcol + q

    def cp_x(s, a, d):
        return pltpu.make_async_remote_copy(
            src_ref=panels.at[a], dst_ref=xch.at[s], send_sem=xssem.at[s, d], recv_sem=xrsem.at[s],
            device_id=((p + d) % n_prow, q), device_id_type=MESH,
        )

    def cp_l(s, a):
        return pltpu.make_async_copy(panels.at[a], xch.at[s], xrsem.at[s])

    def publish(a):
        for s in range(slots):
            g = block_of(s)

            @pl.when((g % n_prow == p) & (g // n_prow == a))
            def _():
                for d in range(1, n_prow):
                    cp_x(s, a, d).start()
                cp_l(s, a).start()

    def wait_slot(s):
        g = block_of(s)

        @pl.when(g % n_prow == p)
        def _():
            cp_l(s, 0).wait()

        @pl.when(g % n_prow != p)
        def _():
            cp_x(s, 0, 1).wait_recv()

    def a_in(a):
        return pltpu.make_async_copy(
            a_hbm.at[pl.ds(pl.multiple_of(a * lines, lines), lines), :], abuf.at[a % 2], asem.at[a % 2])

    def o_out(a):
        return pltpu.make_async_copy(
            obuf.at[a % 2], out_hbm.at[pl.ds(pl.multiple_of(a * lines, lines), lines), :], osem.at[a % 2])

    def s_in(a):
        return pltpu.make_async_copy(
            a_hbm.at[pl.ds(pl.multiple_of(a * lines, lines), lines), :], sbuf.at[a % 2], srcsem.at[a % 2])

    @pl.when(q < STEPS)
    def _():
        s_in(0).start()

    a_in(0).start()

    def const(i):
        return cst[0, i], cst[1, i]

    def solve(ref):
        p0 = dot3(split(ref[0]), const(0))
        s0 = split(p0)
        p1 = dot3(split(ref[1] - dot3(s0, const(3))), const(1))
        s1 = split(p1)
        p2 = dot3(split(ref[2] - dot3(s0, const(4)) - dot3(s1, const(5))), const(2))
        return p0, p1, p2

    def set_const(i, value):
        h, l = split(value)
        cst[0, i] = h
        cst[1, i] = l

    def compute(a):
        g = a * n_prow + p

        @pl.when(a + 1 < rb)
        def _():
            a_in(a + 1).start()

        @pl.when(a == 0)
        def _():
            wait_slot(0)
            wait_slot(1)
            for k in range(STEPS):
                set_const(k, inv_ref[k])
            set_const(3, dot3(split(xch[0, 0]), const(0)))
            set_const(4, dot3(split(xch[1, 0]), const(0)))
            set_const(5, dot3(split(xch[1, 1] - dot3(const(4), const(3))), const(1)))

        parts = solve(panels.at[a])
        for k in range(STEPS):
            v = jnp.where(g >= k, parts[k], 0.0)
            prow_f[k] = v
            h, l = split(v)
            prow_h[0, :, k * nb:(k + 1) * nb] = h
            prow_h[1, :, k * nb:(k + 1) * nb] = l

        for b in range(cb):
            gb = block_of(2 + b)
            first = jnp.minimum((gb - p + n_prow - 1) // n_prow, rb - 1)

            @pl.when(a == first)
            def _():
                wait_slot(2 + b)
                cols = solve(xch.at[2 + b])
                for k in range(STEPS):
                    h, l = split(cols[k])
                    chi[b, :, k * nb:(k + 1) * nb] = h
                    clo[b, :, k * nb:(k + 1) * nb] = l

        @pl.when(a >= 2)
        def _():
            o_out(a - 2).wait()
        a_in(a).wait()
        par = a % 2
        for b in range(cb):
            gb = block_of(2 + b)

            def put(value):
                for h in range(2):
                    obuf[par, pl.ds(b * 2 + h, nb, stride=stride), :] = value[:, h * 128:(h + 1) * 128]

            def updated():
                old = jnp.concatenate(
                    [abuf[par, pl.ds(b * 2 + h, nb, stride=stride), :] for h in range(2)], axis=1)
                return old - dot3((prow_h[0], prow_h[1]), (chi[b], clo[b]))

            @pl.when((gb >= STEPS) & (g > gb))
            def _():
                put(updated())

            @pl.when((gb >= STEPS) & (g == gb))
            def _():
                rows = lax.broadcasted_iota(jnp.int32, (nb, nb), 0)
                cols = lax.broadcasted_iota(jnp.int32, (nb, nb), 1)
                put(jnp.where(rows >= cols, updated(), 0.0))

            @pl.when((gb >= STEPS) & (g < gb))
            def _():
                put(jnp.zeros((nb, nb), F32))

            if b == 0:
                for k in range(STEPS):
                    @pl.when(gb == k)
                    def _():
                        put(prow_f[k])
        o_out(a).start()

    def step(t, carry):
        @pl.when(t < rb)
        def _():
            a = t

            @pl.when(z > 0)
            def _():
                recv_z(a).wait_recv()
                pl.when(z < depth - 1)(lambda: start(send_z, a))
                start(send_x, a)
                start(send_c1, a)

            for k in range(STEPS):
                @pl.when(q == k)
                def _():
                    s_in(a).wait()

                    @pl.when(a + 1 < rb)
                    def _():
                        s_in(a + 1).start()
                    for h in range(2):
                        panels[a, k, :, h * 128:(h + 1) * 128] = sbuf[a % 2, pl.ds(h, nb, stride=stride), :]
                    start(to_x(k), a)
                    start(to_sib(k), a)

        @pl.when((t >= 1) & (t < rb + 1))
        def _():
            a = t - 1

            @pl.when(z > 0)
            def _():
                recv_x(a).wait_recv()
                start(send_c2, a)

            @pl.when(above)
            def _():
                start(send_dn, a)

            for k in range(STEPS):
                @pl.when(q == fwd_of(k))
                def _():
                    fwd(k)(a).wait_recv()
                    start(fwd(k), a)

        @pl.when((t >= 2) & (t < rb + 2))
        def _():
            a = t - 2

            @pl.when(z > 0)
            def _():
                recv_c1(a).wait_recv()
                recv_c2(a).wait_recv()

            @pl.when(z == 0)
            def _():
                for k in range(STEPS):
                    same = k + 1 - 2 * (k % 2)

                    @pl.when(q == same)
                    def _():
                        cp_k(a, k, sib, 1 + 2 * k).wait_recv()

                    @pl.when((q != k) & (q != same) & (q != fwd_of(k)))
                    def _():
                        fwd(k)(a).wait_recv()
                start(send_z, a)

            pl.when(jnp.logical_not(low))(lambda: publish(a))

        @pl.when(low & (t >= 2 + BACK) & (t < rb + 2 + BACK))
        def _():
            a = t - 2 - BACK
            recv_dn(a).wait_recv()
            start(send_dc, a)

        @pl.when(low & (t >= 3 + BACK) & (t < rb + 3 + BACK))
        def _():
            a = t - 3 - BACK
            recv_dc(a).wait_recv()
            publish(a)

        @pl.when((t >= 2 + lag) & (t < rb + 2 + lag))
        def _():
            compute(t - 2 - lag)

        return carry

    lag = jnp.where(low, BACK + 1 + LAG, LAG)
    lax.fori_loop(0, rb + 3 + BACK + LAG, step, 0)

    pl.when(z < depth - 1)(lambda: drain(send_z))

    @pl.when(z > 0)
    def _():
        drain(send_x)
        drain(send_c1)
        drain(send_c2)

    pl.when(above)(lambda: drain(send_dn))
    pl.when(low)(lambda: drain(send_dc))

    for k in range(STEPS):
        @pl.when(q == k)
        def _():
            drain(to_x(k))
            drain(to_sib(k))

        @pl.when(q == fwd_of(k))
        def _():
            drain(fwd(k))
    for s in range(slots):
        @pl.when(block_of(s) % n_prow == p)
        def _():
            for d in range(1, n_prow):
                cp_x(s, 0, d).wait_send()
    for a in range(max(rb - 2, 0), rb):
        o_out(a).wait()


def per_device(n_prow, n_pcol, matrix, inverses):
    rb, _, nb, cb, _, _ = matrix.shape
    lines = matrix.reshape(rb * nb * cb * 2, nb // 2)
    vmem = pltpu.VMEM
    dma = pltpu.SemaphoreType.DMA
    out = pl.pallas_call(
        functools.partial(kernel, n_prow, n_pcol, rb, cb, nb),
        out_shape=jax.ShapeDtypeStruct(lines.shape, F32),
        in_specs=[
            pl.BlockSpec(memory_space=pl.ANY),
            pl.BlockSpec(memory_space=pltpu.VMEM),
        ],
        out_specs=pl.BlockSpec(memory_space=pl.ANY),
        scratch_shapes=[
            vmem((rb, STEPS, nb, nb), F32),
            vmem((2 + cb, STEPS, nb, nb), F32),
            vmem((2, nb * cb * 2, 128), F32),
            vmem((2, nb * cb * 2, 128), F32),
            vmem((2, nb * cb * 2, 128), F32),
            vmem((2, 6, nb, nb), BF),
            vmem((cb, nb, STEPS * nb), BF),
            vmem((cb, nb, STEPS * nb), BF),
            vmem((STEPS, nb, nb), F32),
            vmem((2, nb, STEPS * nb), BF),
            dma((rb, 5)),
            dma((WINDOW, 8)),
            dma((2 + cb,)),
            dma((2 + cb, n_prow)),
            dma((2,)),
            dma((2,)),
            dma((2,)),
        ],
        compiler_params=pltpu.CompilerParams(
            collective_id=0, has_side_effects=True, vmem_limit_bytes=58 * 1024 * 1024
        ),
    )(lines, inverses)
    return out.reshape(matrix.shape)


def solution(mesh):
    in_specs = (P(None, "prow", None, None, "pcol", None), P())
    out_specs = P(None, "prow", None, None, "pcol", None)
    return jax.shard_map(
        functools.partial(per_device, mesh.shape["prow"], mesh.shape["pcol"]),
        mesh=mesh, in_specs=in_specs, out_specs=out_specs, check_vma=False,
    )
```

```python
import functools

import jax
import jax.numpy as jnp
from jax import lax
from jax.experimental import pallas as pl
from jax.experimental.pallas import tpu as pltpu
from jax.sharding import PartitionSpec as P

STEPS = 3
WINDOW = 8
LAG = 2
BACK = 3
MESH = pl.DeviceIdType.MESH
BF = jnp.bfloat16
F32 = jnp.float32


def split(value):
    high = value.astype(BF)
    return high, (value - high.astype(F32)).astype(BF)


def left(value):
    high, low = split(value)
    return jnp.concatenate([high, high, low], axis=1)


def right(value):
    high, low = split(value)
    return jnp.concatenate([high, low, high], axis=0)


def dot(a, b):
    return lax.dot_general(a, b, (((1,), (0,)), ((), ())), preferred_element_type=F32)


def kernel(
    n_prow, n_pcol, rb, cb, nb,
    a_hbm, inv_ref, out_hbm,
    panels, xch, sbuf, abuf, obuf, cst, ccol, prow_f, prow_l,
    rsem, ssem, xrsem, xssem, asem, osem, srcsem,
):
    p = lax.axis_index("prow")
    q = lax.axis_index("pcol")
    depth = n_pcol // 4
    z, x, c = q // 4, (q // 2) % 2, q % 2
    sib = q + 1 - 2 * c
    xn = q + 2 - 4 * x
    quarter = nb // 4
    lines = nb * cb * 2
    stride = cb * 2
    slots = 2 + cb

    barrier = pltpu.get_barrier_semaphore()

    def greet(pp, qq):
        pl.semaphore_signal(barrier, inc=1, device_id=(pp, qq), device_id_type=MESH)

    greet(p, sib)
    greet(p, xn)
    pl.when(z > 0)(lambda: greet(p, q - 4))
    pl.when(z < depth - 1)(lambda: greet(p, q + 4))
    for d in range(1, n_prow):
        greet((p + d) % n_prow, q)
    peers = 1 + n_prow + (z > 0).astype(jnp.int32) + (z < depth - 1).astype(jnp.int32)
    pl.semaphore_wait(barrier, peers)

    def cp_q(a, j, dev, si, ri):
        ref = panels.at[a, :, pl.ds(pl.multiple_of(j * quarter, quarter), quarter), :]
        return pltpu.make_async_remote_copy(
            src_ref=ref, dst_ref=ref, send_sem=ssem.at[a % WINDOW, si], recv_sem=rsem.at[a, ri],
            device_id=(p, dev), device_id_type=MESH,
        )

    def cp_k(a, k, dev, si):
        ref = panels.at[a, k]
        return pltpu.make_async_remote_copy(
            src_ref=ref, dst_ref=ref, send_sem=ssem.at[a % WINDOW, si], recv_sem=rsem.at[a, k],
            device_id=(p, dev), device_id_type=MESH,
        )

    mine = 2 * x + c
    other = 2 * (1 - x) + c
    send_z = lambda a: cp_q(a, mine, jnp.minimum(q + 4, n_pcol - 1), 0, 0)
    send_x = lambda a: cp_q(a, mine, xn, 1, 1)
    send_c1 = lambda a: cp_q(a, mine, sib, 2, 2)
    send_c2 = lambda a: cp_q(a, other, sib, 3, 3)
    recv_z = lambda a: cp_q(a, mine, sib, 0, 0)
    recv_x = lambda a: cp_q(a, other, sib, 1, 1)
    recv_c1 = lambda a: cp_q(a, 2 * x + 1 - c, sib, 2, 2)
    recv_c2 = lambda a: cp_q(a, 2 * (1 - x) + 1 - c, sib, 3, 3)

    def cp_half(a, dev):
        ref = panels.at[a, 0, pl.ds(nb // 2, nb // 2), :]
        return pltpu.make_async_remote_copy(
            src_ref=ref, dst_ref=ref, send_sem=ssem.at[a % WINDOW, 1], recv_sem=rsem.at[a, 0],
            device_id=(p, dev), device_id_type=MESH,
        )

    def cp_dn(a, j, dev, si, ri):
        ref = panels.at[a, 0, pl.ds(pl.multiple_of(j * quarter, quarter), quarter), :]
        return pltpu.make_async_remote_copy(
            src_ref=ref, dst_ref=ref, send_sem=ssem.at[a % WINDOW, si], recv_sem=rsem.at[a, ri],
            device_id=(p, dev), device_id_type=MESH,
        )

    low = (z == 0) & (x == 1)
    above = (z == 1) & (x == 1)
    send_dn = lambda a: cp_dn(a, c, jnp.maximum(q - 4, 0), 4, 3)
    recv_dn = lambda a: cp_dn(a, c, sib, 4, 3)
    send_dc = lambda a: cp_dn(a, c, sib, 7, 4)
    recv_dc = lambda a: cp_dn(a, 1 - c, sib, 7, 4)

    def to_x(k):
        return (lambda i: cp_half(i, xn)) if k == 0 else (lambda i: cp_k(i, k, xn, 1 + 2 * k))

    def to_sib(k):
        return lambda i: cp_k(i, k, sib, 2 + 2 * k)

    def fwd(k):
        return (lambda i: cp_half(i, sib)) if k == 0 else (lambda i: cp_k(i, k, sib, 1 + 2 * k))

    def start(fn, a):
        @pl.when(a >= WINDOW)
        def _():
            fn(a - WINDOW).wait_send()
        fn(a).start()

    def drain(fn):
        for a in range(max(rb - WINDOW, 0), rb):
            fn(a).wait_send()

    def fwd_of(k):
        return k + 2 - 4 * ((k // 2) % 2)

    def block_of(s):
        return s + 1 if s < 2 else (s - 2) * n_pcol + q

    def cp_x(s, a, d):
        return pltpu.make_async_remote_copy(
            src_ref=panels.at[a], dst_ref=xch.at[s], send_sem=xssem.at[s, d], recv_sem=xrsem.at[s],
            device_id=((p + d) % n_prow, q), device_id_type=MESH,
        )

    def cp_l(s, a):
        return pltpu.make_async_copy(panels.at[a], xch.at[s], xrsem.at[s])

    def publish(a):
        for s in range(slots):
            g = block_of(s)

            @pl.when((g % n_prow == p) & (g // n_prow == a))
            def _():
                for d in range(1, n_prow):
                    cp_x(s, a, d).start()
                cp_l(s, a).start()

    def wait_slot(s):
        g = block_of(s)

        @pl.when(g % n_prow == p)
        def _():
            cp_l(s, 0).wait()

        @pl.when(g % n_prow != p)
        def _():
            cp_x(s, 0, 1).wait_recv()

    def a_in(a):
        return pltpu.make_async_copy(
            a_hbm.at[pl.ds(pl.multiple_of(a * lines, lines), lines), :], abuf.at[a % 2], asem.at[a % 2])

    def o_out(a):
        return pltpu.make_async_copy(
            obuf.at[a % 2], out_hbm.at[pl.ds(pl.multiple_of(a * lines, lines), lines), :], osem.at[a % 2])

    def s_in(a):
        return pltpu.make_async_copy(
            a_hbm.at[pl.ds(pl.multiple_of(a * lines, lines), lines), :], sbuf.at[a % 2], srcsem.at[a % 2])

    @pl.when(q < STEPS)
    def _():
        s_in(0).start()

    a_in(0).start()

    def solve(ref):
        parts = jnp.concatenate([left(ref[0]), left(ref[1]), left(ref[2])], axis=1)
        return tuple(dot(parts[:, :(k + 1) * 3 * nb], cst[k, :(k + 1) * 3 * nb, :]) for k in range(STEPS))

    def compute(a):
        g = a * n_prow + p

        @pl.when(a + 1 < rb)
        def _():
            a_in(a + 1).start()

        @pl.when(a == 0)
        def _():
            wait_slot(0)
            wait_slot(1)
            def mul(u, v):
                return dot(left(u), right(v))

            r00, r11, r22 = inv_ref[0].T, inv_ref[1].T, inv_ref[2].T
            w10 = mul(xch[0, 0], r00)
            w20 = mul(xch[1, 0], r00)
            r01 = -mul(mul(r00, w10.T), r11)
            w21 = mul(xch[1, 0], r01) + mul(xch[1, 1], r11)
            r02 = -mul(mul(r00, w20.T) + mul(r01, w21.T), r22)
            r12 = -mul(mul(r11, w21.T), r22)
            for k, column in enumerate(((r00,), (r01, r11), (r02, r12, r22))):
                for m, value in enumerate(column):
                    cst[k, m * 3 * nb:(m + 1) * 3 * nb, :] = right(value)

        parts = solve(panels.at[a])
        for k in range(STEPS):
            v = jnp.where(g >= k, parts[k], 0.0)
            prow_f[k] = v
            prow_l[:, k * 3 * nb:(k + 1) * 3 * nb] = left(v)

        for b in range(cb):
            gb = block_of(2 + b)
            first = jnp.minimum((gb - p + n_prow - 1) // n_prow, rb - 1)

            @pl.when(a == first)
            def _():
                wait_slot(2 + b)
                cols = solve(xch.at[2 + b])
                for k in range(STEPS):
                    ccol[b, k * 3 * nb:(k + 1) * 3 * nb, :] = right(cols[k].T)

        @pl.when(a >= 2)
        def _():
            o_out(a - 2).wait()
        a_in(a).wait()
        par = a % 2
        for b in range(cb):
            gb = block_of(2 + b)

            def put(value):
                for h in range(2):
                    obuf[par, pl.ds(b * 2 + h, nb, stride=stride), :] = value[:, h * 128:(h + 1) * 128]

            def updated():
                old = jnp.concatenate(
                    [abuf[par, pl.ds(b * 2 + h, nb, stride=stride), :] for h in range(2)], axis=1)
                return old - dot(prow_l[...], ccol[b])

            @pl.when((gb >= STEPS) & (g > gb))
            def _():
                put(updated())

            @pl.when((gb >= STEPS) & (g == gb))
            def _():
                rows = lax.broadcasted_iota(jnp.int32, (nb, nb), 0)
                cols = lax.broadcasted_iota(jnp.int32, (nb, nb), 1)
                put(jnp.where(rows >= cols, updated(), 0.0))

            @pl.when((gb >= STEPS) & (g < gb))
            def _():
                put(jnp.zeros((nb, nb), F32))

            if b == 0:
                for k in range(STEPS):
                    @pl.when(gb == k)
                    def _():
                        put(prow_f[k])
        o_out(a).start()

    def step(t, carry):
        @pl.when(t < rb)
        def _():
            a = t

            @pl.when(z > 0)
            def _():
                recv_z(a).wait_recv()
                pl.when(z < depth - 1)(lambda: start(send_z, a))
                start(send_x, a)
                start(send_c1, a)

            for k in range(STEPS):
                @pl.when(q == k)
                def _():
                    s_in(a).wait()

                    @pl.when(a + 1 < rb)
                    def _():
                        s_in(a + 1).start()
                    for h in range(2):
                        panels[a, k, :, h * 128:(h + 1) * 128] = sbuf[a % 2, pl.ds(h, nb, stride=stride), :]
                    start(to_x(k), a)
                    start(to_sib(k), a)

        @pl.when((t >= 1) & (t < rb + 1))
        def _():
            a = t - 1

            @pl.when(z > 0)
            def _():
                recv_x(a).wait_recv()
                start(send_c2, a)

            @pl.when(above)
            def _():
                start(send_dn, a)

            for k in range(STEPS):
                @pl.when(q == fwd_of(k))
                def _():
                    fwd(k)(a).wait_recv()
                    start(fwd(k), a)

        @pl.when((t >= 2) & (t < rb + 2))
        def _():
            a = t - 2

            @pl.when(z > 0)
            def _():
                recv_c1(a).wait_recv()
                recv_c2(a).wait_recv()

            @pl.when(z == 0)
            def _():
                for k in range(STEPS):
                    same = k + 1 - 2 * (k % 2)

                    @pl.when(q == same)
                    def _():
                        cp_k(a, k, sib, 1 + 2 * k).wait_recv()

                    @pl.when((q != k) & (q != same) & (q != fwd_of(k)))
                    def _():
                        fwd(k)(a).wait_recv()
                start(send_z, a)

            pl.when(jnp.logical_not(low))(lambda: publish(a))

        @pl.when(low & (t >= 2 + BACK) & (t < rb + 2 + BACK))
        def _():
            a = t - 2 - BACK
            recv_dn(a).wait_recv()
            start(send_dc, a)

        @pl.when(low & (t >= 3 + BACK) & (t < rb + 3 + BACK))
        def _():
            a = t - 3 - BACK
            recv_dc(a).wait_recv()
            publish(a)

        @pl.when((t >= 2 + lag) & (t < rb + 2 + lag))
        def _():
            compute(t - 2 - lag)

        return carry

    lag = jnp.where(low, BACK + 1 + LAG, LAG)
    lax.fori_loop(0, rb + 3 + BACK + LAG, step, 0)

    pl.when(z < depth - 1)(lambda: drain(send_z))

    @pl.when(z > 0)
    def _():
        drain(send_x)
        drain(send_c1)
        drain(send_c2)

    pl.when(above)(lambda: drain(send_dn))
    pl.when(low)(lambda: drain(send_dc))

    for k in range(STEPS):
        @pl.when(q == k)
        def _():
            drain(to_x(k))
            drain(to_sib(k))

        @pl.when(q == fwd_of(k))
        def _():
            drain(fwd(k))
    for s in range(slots):
        @pl.when(block_of(s) % n_prow == p)
        def _():
            for d in range(1, n_prow):
                cp_x(s, 0, d).wait_send()
    for a in range(max(rb - 2, 0), rb):
        o_out(a).wait()


def per_device(n_prow, n_pcol, matrix, inverses):
    rb, _, nb, cb, _, _ = matrix.shape
    lines = matrix.reshape(rb * nb * cb * 2, nb // 2)
    vmem = pltpu.VMEM
    dma = pltpu.SemaphoreType.DMA
    out = pl.pallas_call(
        functools.partial(kernel, n_prow, n_pcol, rb, cb, nb),
        out_shape=jax.ShapeDtypeStruct(lines.shape, F32),
        in_specs=[
            pl.BlockSpec(memory_space=pl.ANY),
            pl.BlockSpec(memory_space=pltpu.VMEM),
        ],
        out_specs=pl.BlockSpec(memory_space=pl.ANY),
        scratch_shapes=[
            vmem((rb, STEPS, nb, nb), F32),
            vmem((2 + cb, STEPS, nb, nb), F32),
            vmem((2, nb * cb * 2, 128), F32),
            vmem((2, nb * cb * 2, 128), F32),
            vmem((2, nb * cb * 2, 128), F32),
            vmem((STEPS, 3 * STEPS * nb, nb), BF),
            vmem((cb, 3 * STEPS * nb, nb), BF),
            vmem((STEPS, nb, nb), F32),
            vmem((nb, 3 * STEPS * nb), BF),
            dma((rb, 5)),
            dma((WINDOW, 8)),
            dma((2 + cb,)),
            dma((2 + cb, n_prow)),
            dma((2,)),
            dma((2,)),
            dma((2,)),
        ],
        compiler_params=pltpu.CompilerParams(
            collective_id=0, has_side_effects=True, vmem_limit_bytes=58 * 1024 * 1024
        ),
    )(lines, inverses)
    return out.reshape(matrix.shape)


def solution(mesh):
    in_specs = (P(None, "prow", None, None, "pcol", None), P())
    out_specs = P(None, "prow", None, None, "pcol", None)
    return jax.shard_map(
        functools.partial(per_device, mesh.shape["prow"], mesh.shape["pcol"]),
        mesh=mesh, in_specs=in_specs, out_specs=out_specs, check_vma=False,
    )
```
